32 devices in a mesh: expert: 8 (over z, core), width: 4 (over y, x).
Axes of the slice: x: 2, y: 2, z: 4, core: 2. Of those that a mesh axis runs over, the one named last changes fastest.
Arguments:
- up_weights: float32 [32, 4096, 1536], P('expert', 'width'), may hold values from -0.2 to 0.2
- fisher: float32 [32, 4096], P('expert', 'width'), may hold values from 0.1 to 10
- factor_left: float32 [32, 4096, 128], P('expert', 'width'), may hold values from -0.09375 to 0.09375
- factor_right: float32 [32, 128, 1536], P('expert'), may hold values from -0.25 to 0.25
- calib_rows: bfloat16 [8192, 4096], P('expert', 'width'), may hold values from -6 to 6
- routes: int32 [8192, 1], P('expert'), may hold values from 0 to 31; in each aligned block of 1024 rows (0 to 1023, 1024 to 2047, ...) at most 64 rows name the same one
Outputs:
- shared_base: float32 [4096, 1536], P('width')
- residual_out: float32 [8192, 1536], P('expert', 'width')
The draws below stay inside these ranges and needn't reach their ends.
Inputs may be any that keep to these rules, and one draw needn't show every extreme that they name: `routes`: within the rows of one device (each aligned block of 1024 rows) no expert is named by more than 64 rows, a bound that some block reaches.
All inputs are finite; a program needn't handle non-finite values.
Results may differ from the reference program's by a relative error of at most 0.0003.
Values may be sent and summed in bfloat16 or wider, within the bound.
A program may use at most 192 MiB of HBM per device.

```python
import math
import jax
import jax.numpy as jnp
import numpy as np
from jax import lax

D = 4096
F = 1536
RANK = 128
TOK_DEV = 1024
EXPERTS = 32
TOKENS = 8192
CAP = 64
N_EXPERT = 8


def draw_up_weights(key, part):
    key_shared = jax.random.fold_in(key, 11)
    key_own = jax.random.fold_in(key, 12)
    shared_part = jax.random.truncated_normal(key_shared, -6.0, 6.0, (1, D, F), jnp.float32)
    own_part = jax.random.truncated_normal(key_own, -6.0, 6.0, (EXPERTS, D, F), jnp.float32)
    return ((shared_part + 0.5 * own_part) * D ** (-0.5)).astype(jnp.float32)


def block_scale(own_key, dims, split, least, top_value):
    level, own = 1.0, jax.random.fold_in(own_key, 6)
    for position, blocks in split:
        steps = jnp.exp(jax.random.uniform(jax.random.fold_in(own, position), (blocks,), jnp.float32, least / len(split), top_value / len(split)))
        level = level * jnp.repeat(steps, dims[position] // blocks).reshape([-1 if axis == position else 1 for axis in range(len(dims))])
    return level


def deal_out(own_key, own, number, rows, number_of, top, reach, slope):
    ranking = jax.random.permutation(own_key, number_of)
    crowded, common = shares(number_of, rows * top, reach, slope, True), shares(number_of, rows * top, reach, slope, False)
    places = jnp.arange(number_of)

    def named(tallies, offset_by):
        used = int((tallies > 0).sum())
        fixed = max(1, used // 4)
        passed = fixed + (places - fixed + offset_by * (used - fixed)) % max(1, number_of - fixed)
        return jnp.zeros((number_of,), jnp.int32).at[ranking[jnp.where(places < fixed, places, passed)]].set(jnp.asarray(tallies, jnp.int32))

    tallies = jnp.where(number % 4 == 0, named(crowded, number // 4), named(common, number - number // 4 - 1))
    mixed = jax.random.permutation(jax.random.fold_in(own, 3), number_of)
    donor, sink = mixed[0:number_of // 2 * 2:2], mixed[1:number_of // 2 * 2:2]
    margin = jnp.minimum(tallies[donor] - 1, reach - tallies[sink]) // 2
    margin = jnp.where((donor == ranking[0]) | (sink == ranking[0]) | (tallies[sink] == 0), 0, jnp.maximum(margin, 0))
    passed = jax.random.randint(jax.random.fold_in(own, 4), (number_of // 2,), 0, 1 << 20) % (margin + 1)
    tallies = tallies.at[donor].add(-passed).at[sink].add(passed)
    labels = jnp.searchsorted(jnp.cumsum(tallies), jnp.arange(rows * top), side="right").astype(jnp.int32)
    grid = labels.reshape(top, rows).T
    grid = grid[jax.random.permutation(jax.random.fold_in(own, 1), rows)]
    offset_by = jax.random.randint(jax.random.fold_in(own, 2), (rows, 1), 0, top)
    return jnp.take_along_axis(grid, (jnp.arange(top)[None, :] + offset_by) % top, axis=1)


def shares(count, total, bound, slope, full):
    portions = [(1 << 20) // math.isqrt(standing ** slope) + 1 for standing in range(1, count + 1)]
    largest = bound if full else min(bound, max(-(-total // count), total * portions[0] // sum(portions)))
    least = 1 if total - largest >= count - 1 else 0
    given, rest = [largest] + [least] * (count - 1), total - largest - least * (count - 1)
    while rest > 0:
        movable = [i for i in range(1, count) if given[i] < largest] or [i for i in range(1, count) if given[i] < bound]
        pool, remaining = sum([portions[i] for i in movable]), rest
        for i in movable:
            addition = min(bound - given[i], max(1, remaining * portions[i] // pool), rest)
            given[i] = given[i] + addition
            rest = rest - addition
    return np.array(given)


def noise(key, shape, deviation, reach, split=(), kind=jnp.bfloat16):
    drawn = deviation * jax.random.normal(key, shape, jnp.float32)
    if split:
        drawn = drawn * block_scale(key, shape, split, -0.22, 0.18)
    return jnp.clip(drawn, -reach, reach).astype(kind)


def setup_inputs(seed: int = 0) -> dict:
    seeds = jax.random.split(jax.random.key(seed), 7)
    up_weights = draw_up_weights(jax.random.fold_in(seeds[6], 71), 0)
    fisher = jnp.clip(jnp.exp(math.log(10.0) - 4.6051702 * jax.random.uniform(seeds[1], (EXPERTS, D), jnp.float32) ** block_scale(seeds[1], (EXPERTS, D), ((0, 8), (1, 4)), -0.2, 0.2)), 0.1, 10.0)
    factor_left = noise(seeds[2], (EXPERTS, D, RANK), D ** -0.5, 0.09375, ((0, 8), (1, 4)), jnp.float32)
    factor_right = noise(seeds[3], (EXPERTS, RANK, F), (4 * RANK) ** -0.5, 0.25, ((0, 8),), jnp.float32)
    calib_rows = noise(seeds[4], (TOKENS, D), 1.0, 6.0, ((0, 8), (1, 4)))
    routes_keys = jax.random.split(jax.random.fold_in(seeds[5], 1), TOKENS // TOK_DEV)
    routes_turns = jax.random.permutation(jax.random.fold_in(seeds[5], 3), TOKENS // TOK_DEV)
    routes = jax.vmap(lambda own, number: deal_out(jax.random.fold_in(seeds[5], 2), own, number, TOK_DEV, EXPERTS, 1, CAP, 2))(routes_keys, routes_turns).reshape((TOKENS, 1))
    return dict(up_weights=up_weights, fisher=fisher, factor_left=factor_left, factor_right=factor_right, calib_rows=calib_rows, routes=routes)


def reference(up_weights, fisher, factor_left, factor_right, calib_rows, routes):
    weight_total = jnp.sum(fisher, axis=0)
    weighted_sum = jnp.einsum("ed,edf->df", fisher, up_weights, precision=lax.Precision.HIGHEST)
    shared_base = weighted_sum / weight_total[:, None]
    route_ids = routes[:, 0]
    most_rows = CAP * N_EXPERT

    def one_expert(accumulated, expert_id):
        chosen_rows = jnp.argsort((route_ids != expert_id).astype(jnp.int32), stable=True)[:most_rows]
        low_rank = jnp.dot(factor_left[expert_id], factor_right[expert_id], precision=lax.Precision.HIGHEST)
        residual = up_weights[expert_id] - shared_base - low_rank
        picked = calib_rows[chosen_rows].astype(jnp.float32)
        product = jnp.dot(picked, residual, precision=lax.Precision.HIGHEST)
        is_live = route_ids[chosen_rows] == expert_id
        accumulated = accumulated.at[chosen_rows].add(jnp.where(is_live[:, None], product, jnp.zeros_like(product)))
        return accumulated, None

    start = jnp.zeros((calib_rows.shape[0], F), jnp.float32)
    result, unused = lax.scan(one_expert, start, jnp.arange(EXPERTS, dtype=jnp.int32))
    return shared_base, result
```

```python
import functools

import jax
import jax.numpy as jnp
from jax import lax
from jax.experimental import pallas as pl
from jax.experimental.pallas import tpu as pltpu
from jax.sharding import PartitionSpec as P

PAD = 16
CHUNKS = 2


def encode(values, axis):
    top = jnp.max(jnp.abs(values), axis=axis, keepdims=True)
    code = jnp.ceil(jnp.log2(jnp.maximum(top, 1e-30)) * 256.0)
    level = jnp.round(values * (32767.0 * jnp.exp2(code * (-1.0 / 256.0))))
    level = jnp.clip(level, -32767.0, 32767.0)
    return level.astype(jnp.int32).astype(jnp.int16), code.astype(jnp.int32).astype(jnp.int16)


def step_of(code):
    return jnp.exp2(code.astype(jnp.float32) * (1.0 / 256.0)) * (1.0 / 32767.0)


def split(x):
    high = x.astype(jnp.bfloat16)
    return high, (x - high.astype(jnp.float32)).astype(jnp.bfloat16)


def product_kernel(rows_ref, up_ref, base_ref, left_ref, right_ref, out_ref):
    dot = functools.partial(jnp.dot, preferred_element_type=jnp.float32)
    left_high, left_low = split(left_ref[0])
    right_high, right_low = split(right_ref[0])
    low_rank = dot(left_high, right_high) + (dot(left_high, right_low) + dot(left_low, right_high))
    high, low = split(up_ref[0] - base_ref[...] - low_rank)
    groups, _, capacity, width_rows = rows_ref.shape
    rows = rows_ref[...].reshape(groups * capacity, width_rows)
    value = dot(rows, high) + dot(rows, low)
    level, code = encode(value, 0)
    out_ref[0, 0, : groups * capacity, :] = level
    out_ref[0, 0, groups * capacity :, :] = jnp.broadcast_to(code.astype(jnp.int32), (PAD, value.shape[1])).astype(jnp.int16)


def product(rows, up, base, left, right, first, parts):
    groups, count, capacity, width_rows = rows.shape
    hidden = up.shape[2]
    rank = left.shape[2]
    block = hidden // parts
    if block % 128:
        parts, block = 1, hidden
    total = groups * capacity
    return pl.pallas_call(
        product_kernel,
        grid=(count, parts),
        in_specs=[
            pl.BlockSpec((groups, 1, capacity, width_rows), lambda e, f: (0, e, 0, 0)),
            pl.BlockSpec((1, width_rows, block), lambda e, f: (first + e, 0, f)),
            pl.BlockSpec((width_rows, block), lambda e, f: (0, f)),
            pl.BlockSpec((1, width_rows, rank), lambda e, f: (first + e, 0, 0)),
            pl.BlockSpec((1, rank, block), lambda e, f: (first + e, 0, f)),
        ],
        out_specs=pl.BlockSpec((1, 1, total + PAD, block), lambda e, f: (f, e, 0, 0)),
        out_shape=jax.ShapeDtypeStruct((parts, count, total + PAD, block), jnp.int16),
        cost_estimate=pl.CostEstimate(
            flops=4 * count * total * width_rows * hidden,
            bytes_accessed=count * (8 * width_rows * hidden + 2 * total * (width_rows + hidden)),
            transcendentals=0,
        ),
        name="product",
    )(rows, up, base, left, right)


def local(up_weights, fisher, factor_left, factor_right, calib_rows, routes):
    exp_local, width_rows, hidden = up_weights.shape
    groups = lax.axis_size("expert")
    parts = lax.axis_size("width")
    expert_total = exp_local * groups
    tok_rows = calib_rows.shape[0]
    capacity = 2 * tok_rows // expert_total
    slots = expert_total * capacity
    block = hidden // parts

    total_local = jnp.sum(fisher, axis=0)
    weighted = fisher[0][:, None] * up_weights[0]
    for e in range(1, exp_local):
        weighted = weighted + fisher[e][:, None] * up_weights[e]
    weight_total = lax.psum_scatter(total_local, "expert", scatter_dimension=0, tiled=True)
    shard = lax.psum_scatter(weighted, "expert", scatter_dimension=0, tiled=True)
    shard = shard / weight_total[:, None]
    level, code = encode(shard, 0)
    packed = jnp.concatenate([level, jnp.broadcast_to(code, (PAD, hidden))], axis=0)
    packed = lax.all_gather(packed, "expert", axis=0)
    keep = shard.shape[0]
    shared_base = packed[:, :keep].astype(jnp.float32) * step_of(packed[:, keep : keep + 1])
    shared_base = shared_base.reshape(width_rows, hidden)

    route_ids = routes[:, 0]
    one_hot = route_ids[:, None] == jnp.arange(expert_total, dtype=jnp.int32)[None, :]
    before = jnp.arange(tok_rows)[:, None] > jnp.arange(tok_rows)[None, :]
    earlier = jnp.dot(
        before.astype(jnp.bfloat16), one_hot.astype(jnp.bfloat16), preferred_element_type=jnp.float32
    )
    slot_index = jnp.sum(jnp.where(one_hot, earlier, 0.0), axis=1).astype(jnp.int32)
    step = exp_local // CHUNKS
    target = route_ids * capacity + slot_index
    owner, inner = route_ids // exp_local, route_ids % exp_local

    returned = []
    for c in range(CHUNKS):
        first = c * step
        place = jnp.arange(groups * step * capacity, dtype=jnp.int32)
        spot = (place // (step * capacity)) * (exp_local * capacity) + first * capacity + place % (step * capacity)
        chosen = (spot[:, None] == target[None, :]).astype(jnp.bfloat16)
        outgoing = jnp.dot(chosen, calib_rows, preferred_element_type=jnp.float32).astype(jnp.bfloat16)
        outgoing = outgoing.reshape(groups, step * capacity, width_rows)
        incoming = lax.all_to_all(outgoing, "expert", split_axis=0, concat_axis=0, tiled=True)
        incoming = incoming.reshape(groups, step, capacity, width_rows)
        value = product(incoming, up_weights, shared_base, factor_left, factor_right, first, parts)
        if value.shape[0] != parts:
            value = value[0].reshape(step, -1, parts, block).transpose(2, 0, 1, 3)
        value = lax.all_to_all(value, "width", split_axis=0, concat_axis=0, tiled=True)
        rows_all = groups * capacity
        summed = jnp.sum(
            value[:, :, :rows_all].astype(jnp.float32) * step_of(value[:, :, rows_all : rows_all + 1]), axis=0
        )
        summed = summed.reshape(step, groups, capacity, block).transpose(1, 0, 2, 3)
        summed = summed.reshape(groups, step * capacity, block)
        level, code = encode(summed, 1)
        back = jnp.concatenate([level, jnp.broadcast_to(code, (groups, PAD, block))], axis=1)
        back = lax.all_to_all(back, "expert", split_axis=0, concat_axis=0, tiled=True)
        home = back[:, : step * capacity].astype(jnp.float32) * step_of(back[:, step * capacity : step * capacity + 1])
        returned.append(home.reshape(groups * step * capacity, block))
    returned = jnp.concatenate(returned, axis=0)
    chunk, within = inner // step, inner % step
    where = ((chunk * groups + owner) * step + within) * capacity + slot_index
    return (shared_base, returned[where])


def solution(mesh):
    placed = (
        P("expert", "width", None),
        P("expert", "width"),
        P("expert", "width", None),
        P("expert", None, None),
        P("expert", "width"),
        P("expert", None),
    )
    return jax.shard_map(
        local,
        mesh=mesh,
        in_specs=placed,
        out_specs=(P("width", None), P("expert", "width")),
        check_vma=False,
    )
```

```python
import functools

import jax
import jax.numpy as jnp
from jax import lax
from jax.experimental import pallas as pl
from jax.experimental.pallas import tpu as pltpu
from jax.sharding import PartitionSpec as P

PAD = 16
CHUNKS = 2


def encode(values, axis):
    top = jnp.max(jnp.abs(values), axis=axis, keepdims=True)
    code = jnp.ceil(jnp.log2(jnp.maximum(top, 1e-30)) * 256.0)
    level = jnp.round(values * (32767.0 * jnp.exp2(code * (-1.0 / 256.0))))
    level = jnp.clip(level, -32767.0, 32767.0)
    return level.astype(jnp.int32).astype(jnp.int16), code.astype(jnp.int32).astype(jnp.int16)


def step_of(code):
    return jnp.exp2(code.astype(jnp.float32) * (1.0 / 256.0)) * (1.0 / 32767.0)


def split(x):
    high = x.astype(jnp.bfloat16)
    return high, (x - high.astype(jnp.float32)).astype(jnp.bfloat16)


def product_kernel(rows_ref, up_ref, base_ref, left_ref, right_ref, out_ref):
    dot = functools.partial(jnp.dot, preferred_element_type=jnp.float32)
    left_high, left_low = split(left_ref[0])
    right_high, right_low = split(right_ref[0])
    low_rank = dot(left_high, right_high) + (dot(left_high, right_low) + dot(left_low, right_high))
    high, low = split(up_ref[0] - base_ref[...] - low_rank)
    groups, _, capacity, width_rows = rows_ref.shape
    rows = rows_ref[...].reshape(groups * capacity, width_rows)
    value = dot(rows, high) + dot(rows, low)
    level, code = encode(value, 0)
    out_ref[0, : groups * capacity, :] = level
    out_ref[0, groups * capacity :, :] = jnp.broadcast_to(code.astype(jnp.int32), (PAD, value.shape[1])).astype(jnp.int16)


def product(rows, up, base, left, right, first, inside, parts):
    groups, _, capacity, width_rows = rows.shape
    hidden = up.shape[2]
    rank = left.shape[2]
    block = hidden // parts
    if block % 128:
        parts, block = 1, hidden
    total = groups * capacity
    return pl.pallas_call(
        product_kernel,
        grid=(parts,),
        in_specs=[
            pl.BlockSpec((groups, 1, capacity, width_rows), lambda f: (0, inside, 0, 0)),
            pl.BlockSpec((1, width_rows, block), lambda f: (first + inside, 0, f)),
            pl.BlockSpec((width_rows, block), lambda f: (0, f)),
            pl.BlockSpec((1, width_rows, rank), lambda f: (first + inside, 0, 0)),
            pl.BlockSpec((1, rank, block), lambda f: (first + inside, 0, f)),
        ],
        out_specs=pl.BlockSpec((1, total + PAD, block), lambda f: (f, 0, 0)),
        out_shape=jax.ShapeDtypeStruct((parts, total + PAD, block), jnp.int16),
        cost_estimate=pl.CostEstimate(
            flops=4 * total * width_rows * hidden,
            bytes_accessed=8 * width_rows * hidden + 2 * total * (width_rows + hidden),
            transcendentals=0,
        ),
        name="product",
    )(rows, up, base, left, right)


def width_sum(value, rows):
    parts = value.shape[0]
    me = lax.axis_index("width")

    def opened(piece):
        return piece[:rows].astype(jnp.float32) * step_of(piece[rows : rows + 1])

    sent = []
    for k in range(1, parts):
        piece = lax.dynamic_index_in_dim(value, me ^ k, 0, keepdims=False)
        sent.append(lax.ppermute(piece, "width", [(i, i ^ k) for i in range(parts)]))
    total = opened(lax.dynamic_index_in_dim(value, me, 0, keepdims=False))
    for piece in sent:
        total = total + opened(piece)
    return total


def local(up_weights, fisher, factor_left, factor_right, calib_rows, routes):
    exp_local, width_rows, hidden = up_weights.shape
    groups = lax.axis_size("expert")
    parts = lax.axis_size("width")
    expert_total = exp_local * groups
    tok_rows = calib_rows.shape[0]
    capacity = 2 * tok_rows // expert_total
    slots = expert_total * capacity
    block = hidden // parts

    total_local = jnp.sum(fisher, axis=0)
    weighted = fisher[0][:, None] * up_weights[0]
    for e in range(1, exp_local):
        weighted = weighted + fisher[e][:, None] * up_weights[e]
    joined = jnp.concatenate([weighted, jnp.broadcast_to(total_local[:, None], (width_rows, 128))], axis=1)
    joined = lax.psum_scatter(joined, "expert", scatter_dimension=0, tiled=True)
    shard = joined[:, :hidden] / joined[:, hidden : hidden + 1]
    level, code = encode(shard, 0)
    packed = jnp.concatenate([level, jnp.broadcast_to(code, (PAD, hidden))], axis=0)
    packed = lax.all_gather(packed, "expert", axis=0)
    keep = shard.shape[0]
    shared_base = packed[:, :keep].astype(jnp.float32) * step_of(packed[:, keep : keep + 1])
    shared_base = shared_base.reshape(width_rows, hidden)

    route_ids = routes[:, 0]
    one_hot = route_ids[:, None] == jnp.arange(expert_total, dtype=jnp.int32)[None, :]
    before = jnp.arange(tok_rows)[:, None] > jnp.arange(tok_rows)[None, :]
    earlier = jnp.dot(
        before.astype(jnp.bfloat16), one_hot.astype(jnp.bfloat16), preferred_element_type=jnp.float32
    )
    slot_index = jnp.sum(jnp.where(one_hot, earlier, 0.0), axis=1).astype(jnp.int32)
    step = exp_local // CHUNKS
    target = route_ids * capacity + slot_index
    owner, inner = route_ids // exp_local, route_ids % exp_local

    returned = []
    for c in range(CHUNKS):
        first = c * step
        place = jnp.arange(groups * step * capacity, dtype=jnp.int32)
        spot = (place // (step * capacity)) * (exp_local * capacity) + first * capacity + place % (step * capacity)
        chosen = (spot[:, None] == target[None, :]).astype(jnp.bfloat16)
        outgoing = jnp.dot(chosen, calib_rows, preferred_element_type=jnp.float32).astype(jnp.bfloat16)
        outgoing = outgoing.reshape(groups, step * capacity, width_rows)
        incoming = lax.all_to_all(outgoing, "expert", split_axis=0, concat_axis=0, tiled=True)
        incoming = incoming.reshape(groups, step, capacity, width_rows)
        for inside in range(step):
            value = product(incoming, up_weights, shared_base, factor_left, factor_right, first, inside, parts)
            if value.shape[0] != parts:
                value = value[0].reshape(-1, parts, block).transpose(1, 0, 2)
            summed = width_sum(value, groups * capacity)
            level, code = encode(summed.reshape(groups, capacity, block), 1)
            back = jnp.concatenate([level, jnp.broadcast_to(code, (groups, PAD, block))], axis=1)
            back = lax.all_to_all(back, "expert", split_axis=0, concat_axis=0, tiled=True)
            home = back[:, :capacity].astype(jnp.float32) * step_of(back[:, capacity : capacity + 1])
            returned.append(home.reshape(groups * capacity, block))
    returned = jnp.concatenate(returned, axis=0)
    where = (inner * groups + owner) * capacity + slot_index
    return (shared_base, returned[where])


def solution(mesh):
    placed = (
        P("expert", "width", None),
        P("expert", "width"),
        P("expert", "width", None),
        P("expert", None, None),
        P("expert", "width"),
        P("expert", None),
    )
    return jax.shard_map(
        local,
        mesh=mesh,
        in_specs=placed,
        out_specs=(P("width", None), P("expert", "width")),
        check_vma=False,
    )
```

```python
import functools

import jax
import jax.numpy as jnp
from jax import lax
from jax.experimental import pallas as pl
from jax.experimental.pallas import tpu as pltpu
from jax.sharding import PartitionSpec as P

PAD = 16
CHUNKS = 2


def encode(values, axis):
    top = jnp.max(jnp.abs(values), axis=axis, keepdims=True)
    code = jnp.ceil(jnp.log2(jnp.maximum(top, 1e-30)) * 256.0)
    level = jnp.round(values * (32767.0 * jnp.exp2(code * (-1.0 / 256.0))))
    level = jnp.clip(level, -32767.0, 32767.0)
    return level.astype(jnp.int32).astype(jnp.int16), code.astype(jnp.int32).astype(jnp.int16)


def step_of(code):
    return jnp.exp2(code.astype(jnp.float32) * (1.0 / 256.0)) * (1.0 / 32767.0)


def split(x):
    high = x.astype(jnp.bfloat16)
    return high, (x - high.astype(jnp.float32)).astype(jnp.bfloat16)


def product_kernel(rows_ref, up_ref, base_ref, left_ref, right_ref, out_ref):
    dot = functools.partial(jnp.dot, preferred_element_type=jnp.float32)
    left_high, left_low = split(left_ref[0])
    right_high, right_low = split(right_ref[0])
    low_rank = dot(left_high, right_high) + (dot(left_high, right_low) + dot(left_low, right_high))
    high, low = split(up_ref[0] - base_ref[...] - low_rank)
    groups, _, capacity, width_rows = rows_ref.shape
    rows = rows_ref[...].reshape(groups * capacity, width_rows)
    value = dot(rows, high) + dot(rows, low)
    level, code = encode(value, 0)
    out_ref[0, : groups * capacity, :] = level
    out_ref[0, groups * capacity :, :] = jnp.broadcast_to(code.astype(jnp.int32), (PAD, value.shape[1])).astype(jnp.int16)


def product(rows, up, base, left, right, first, inside, parts):
    groups, _, capacity, width_rows = rows.shape
    hidden = up.shape[2]
    rank = left.shape[2]
    block = hidden // parts
    if block % 128:
        parts, block = 1, hidden
    total = groups * capacity
    return pl.pallas_call(
        product_kernel,
        grid=(parts,),
        in_specs=[
            pl.BlockSpec((groups, 1, capacity, width_rows), lambda f: (0, inside, 0, 0)),
            pl.BlockSpec((1, width_rows, block), lambda f: (first + inside, 0, f)),
            pl.BlockSpec((width_rows, block), lambda f: (0, f)),
            pl.BlockSpec((1, width_rows, rank), lambda f: (first + inside, 0, 0)),
            pl.BlockSpec((1, rank, block), lambda f: (first + inside, 0, f)),
        ],
        out_specs=pl.BlockSpec((1, total + PAD, block), lambda f: (f, 0, 0)),
        out_shape=jax.ShapeDtypeStruct((parts, total + PAD, block), jnp.int16),
        cost_estimate=pl.CostEstimate(
            flops=4 * total * width_rows * hidden,
            bytes_accessed=8 * width_rows * hidden + 2 * total * (width_rows + hidden),
            transcendentals=0,
        ),
        name="product",
    )(rows, up, base, left, right)


def width_sum(value, rows):
    parts = value.shape[0]
    me = lax.axis_index("width")

    def opened(piece):
        return piece[:rows].astype(jnp.float32) * step_of(piece[rows : rows + 1])

    sent = []
    for k in range(1, parts):
        piece = lax.dynamic_index_in_dim(value, me ^ k, 0, keepdims=False)
        sent.append(lax.ppermute(piece, "width", [(i, i ^ k) for i in range(parts)]))
    total = opened(lax.dynamic_index_in_dim(value, me, 0, keepdims=False))
    for piece in sent:
        total = total + opened(piece)
    return total


def local(up_weights, fisher, factor_left, factor_right, calib_rows, routes):
    exp_local, width_rows, hidden = up_weights.shape
    groups = lax.axis_size("expert")
    parts = lax.axis_size("width")
    expert_total = exp_local * groups
    tok_rows = calib_rows.shape[0]
    capacity = 2 * tok_rows // expert_total
    slots = expert_total * capacity
    block = hidden // parts

    total_local = jnp.sum(fisher, axis=0)
    weighted = fisher[0][:, None] * up_weights[0]
    for e in range(1, exp_local):
        weighted = weighted + fisher[e][:, None] * up_weights[e]
    me = lax.axis_index("expert")
    chips, chip, core = groups // 2, me // 2, me % 2
    keep = width_rows // groups
    pick = functools.partial(lax.dynamic_index_in_dim, keepdims=False)
    partner = [(i, i ^ 1) for i in range(groups)]

    def beside(block):
        return pick(block, core, 1) + lax.ppermute(pick(block, 1 - core, 1), "expert", partner)

    sums = beside(weighted.reshape(chips, 2, keep, hidden))
    totals = beside(total_local.reshape(chips, 2, keep))
    sums_level, sums_code = encode(sums, 1)
    sums_packed = jnp.concatenate([sums_level, jnp.broadcast_to(sums_code, (chips, PAD, hidden))], axis=1)
    shard, weight_total = pick(sums, chip, 0), pick(totals, chip, 0)
    hops = [[(i, i ^ (2 * k)) for i in range(groups)] for k in range(1, chips)]
    for k, hop in enumerate(hops, 1):
        piece = lax.ppermute(pick(sums_packed, chip ^ k, 0), "expert", hop)
        shard = shard + piece[:keep].astype(jnp.float32) * step_of(piece[keep : keep + 1])
        weight_total = weight_total + lax.ppermute(pick(totals, chip ^ k, 0), "expert", hop)
    shard = shard / weight_total[:, None]
    level, code = encode(shard, 0)
    packed = jnp.concatenate([level, jnp.broadcast_to(code, (PAD, hidden))], axis=0)
    mine = jnp.stack([packed] + [lax.ppermute(packed, "expert", hop) for hop in hops])
    other = lax.ppermute(mine, "expert", partner)
    first_core, second_core = jnp.where(core == 0, mine, other), jnp.where(core == 0, other, mine)
    pairs = jnp.stack([first_core, second_core], axis=1)
    packed = jnp.stack([pick(pairs, chip ^ z, 0) for z in range(chips)]).reshape(groups, keep + PAD, hidden)
    shared_base = packed[:, :keep].astype(jnp.float32) * step_of(packed[:, keep : keep + 1])
    shared_base = shared_base.reshape(width_rows, hidden)

    route_ids = routes[:, 0]
    one_hot = route_ids[:, None] == jnp.arange(expert_total, dtype=jnp.int32)[None, :]
    before = jnp.arange(tok_rows)[:, None] > jnp.arange(tok_rows)[None, :]
    earlier = jnp.dot(
        before.astype(jnp.bfloat16), one_hot.astype(jnp.bfloat16), preferred_element_type=jnp.float32
    )
    slot_index = jnp.sum(jnp.where(one_hot, earlier, 0.0), axis=1).astype(jnp.int32)
    step = exp_local // CHUNKS
    target = route_ids * capacity + slot_index
    owner, inner = route_ids // exp_local, route_ids % exp_local

    returned = []
    for c in range(CHUNKS):
        first = c * step
        place = jnp.arange(groups * step * capacity, dtype=jnp.int32)
        spot = (place // (step * capacity)) * (exp_local * capacity) + first * capacity + place % (step * capacity)
        chosen = (spot[:, None] == target[None, :]).astype(jnp.bfloat16)
        outgoing = jnp.dot(chosen, calib_rows, preferred_element_type=jnp.float32).astype(jnp.bfloat16)
        outgoing = outgoing.reshape(groups, step * capacity, width_rows)
        incoming = lax.all_to_all(outgoing, "expert", split_axis=0, concat_axis=0, tiled=True)
        incoming = incoming.reshape(groups, step, capacity, width_rows)
        for inside in range(step):
            value = product(incoming, up_weights, shared_base, factor_left, factor_right, first, inside, parts)
            if value.shape[0] != parts:
                value = value[0].reshape(-1, parts, block).transpose(1, 0, 2)
            summed = width_sum(value, groups * capacity)
            level, code = encode(summed.reshape(groups, capacity, block), 1)
            back = jnp.concatenate([level, jnp.broadcast_to(code, (groups, PAD, block))], axis=1)
            back = lax.all_to_all(back, "expert", split_axis=0, concat_axis=0, tiled=True)
            home = back[:, :capacity].astype(jnp.float32) * step_of(back[:, capacity : capacity + 1])
            returned.append(home.reshape(groups * capacity, block))
    returned = jnp.concatenate(returned, axis=0)
    where = (inner * groups + owner) * capacity + slot_index
    return (shared_base, returned[where])


def solution(mesh):
    placed = (
        P("expert", "width", None),
        P("expert", "width"),
        P("expert", "width", None),
        P("expert", None, None),
        P("expert", "width"),
        P("expert", None),
    )
    return jax.shard_map(
        local,
        mesh=mesh,
        in_specs=placed,
        out_specs=(P("width", None), P("expert", "width")),
        check_vma=False,
    )
```
